32 devices in a mesh: row: 8 (over z, x), col: 2 (over y), depth: 2 (over core).
Axes of the slice: x: 2, y: 2, z: 4, core: 2. Of those that a mesh axis runs over, the one named last changes fastest.
Arguments:
- volume: bfloat16 [16, 32, 16, 256], P('row', 'col', 'depth'), may hold values from -6 to 6
- first_kernel: bfloat16 [27, 256, 256], P(None, 'row'), may hold values from -0.078125 to 0.078125
- down_kernel: bfloat16 [8, 256, 512], replicated, may hold values from -0.125 to 0.125
- mid_kernel: bfloat16 [27, 512, 512], P(None, None, 'col'), may hold values from -0.0546875 to 0.0546875
- up_kernel: bfloat16 [8, 512, 256], replicated, may hold values from -0.25 to 0.25
- last_kernel: bfloat16 [27, 512, 256], P(None, 'row'), may hold values from -0.0546875 to 0.0546875
Outputs:
- decoded: bfloat16 [16, 32, 16, 256], P('row', 'col', 'depth')
The draws below stay inside these ranges and needn't reach their ends.
All inputs are finite; a program needn't handle non-finite values.
Results may differ from the reference program's by a relative error of at most 0.0055.
Values may be sent and summed in bfloat16 or wider, within the bound.
A program may use at most 64 MiB of HBM per device.

```python
import jax
import jax.numpy as jnp
from jax import lax

CHANS = 256
WIDE = 512
ROWS = 16
COLS = 32
DEEP = 16


def block_scale(rng, shape, split, low, largest):
    def one(axis_at, parts):
        heights = jax.random.uniform(jax.random.fold_in(jax.random.fold_in(rng, 6), axis_at), (parts,), jnp.float32, low / len(split), largest / len(split))
        return jnp.repeat(jnp.exp(heights), shape[axis_at] // parts).reshape((-1,) + (1,) * (len(shape) - axis_at - 1))

    loudness = one(*split[0])
    for cut in split[1:]:
        loudness = loudness * one(*cut)
    return loudness


def bell_draw(key, extent, width, bound, cuts=(), kind=jnp.bfloat16):
    gain = block_scale(key, extent, cuts, -0.22, 0.18) if cuts else 1.0
    values = jax.random.normal(key, extent, jnp.float32) * width * gain
    return jnp.minimum(jnp.maximum(values, -bound), bound).astype(kind)


def setup_inputs(seed: int = 0) -> dict:
    seeds = jax.random.split(jax.random.key(seed), 7)
    return {
        "volume": bell_draw(seeds[0], (ROWS, COLS, DEEP, CHANS), 1.0, 6.0, ((0, 8), (1, 2), (2, 2))),
        "first_kernel": bell_draw(seeds[1], (27, CHANS, CHANS), (27 * CHANS) ** -0.5, 0.078125, ((1, 8),)),
        "down_kernel": bell_draw(seeds[2], (8, CHANS, WIDE), (8 * CHANS) ** -0.5, 0.125),
        "mid_kernel": bell_draw(seeds[3], (27, WIDE, WIDE), (27 * WIDE) ** -0.5, 0.0546875, ((2, 2),)),
        "up_kernel": bell_draw(seeds[4], (8, WIDE, CHANS), WIDE ** -0.5, 0.25),
        "last_kernel": bell_draw(seeds[5], (27, 2 * CHANS, CHANS), (27 * 2 * CHANS) ** -0.5, 0.0546875, ((1, 8),)),
    }


def conv_same(volume_in, weight):
    kernel = weight.reshape(3, 3, 3, weight.shape[1], weight.shape[2])
    result = lax.conv_general_dilated(volume_in[None], kernel, (1, 1, 1), ((1, 1), (1, 1), (1, 1)), dimension_numbers=("NDHWC", "DHWIO", "NDHWC"), preferred_element_type=jnp.float32)
    return result[0]


def reference(volume, first_kernel, down_kernel, mid_kernel, up_kernel, last_kernel):
    skip = jax.nn.gelu(conv_same(volume, first_kernel)).astype(jnp.bfloat16)
    down_weights = down_kernel.reshape(2, 2, 2, down_kernel.shape[1], down_kernel.shape[2])
    coarse_raw = lax.conv_general_dilated(skip[None], down_weights, (2, 2, 2), "VALID", dimension_numbers=("NDHWC", "DHWIO", "NDHWC"), preferred_element_type=jnp.float32)[0]
    coarse = jax.nn.gelu(coarse_raw).astype(jnp.bfloat16)
    middle = jax.nn.gelu(conv_same(coarse, mid_kernel)).astype(jnp.bfloat16)
    coarse_x, coarse_y, coarse_z, wide_chans = middle.shape
    fine_chans = up_kernel.shape[2]
    up_table = jnp.transpose(up_kernel, (1, 0, 2)).reshape(wide_chans, 8 * fine_chans)
    lifted_flat = jnp.dot(middle.reshape(-1, wide_chans), up_table, preferred_element_type=jnp.float32).astype(jnp.bfloat16)
    lifted = lifted_flat.reshape(coarse_x, coarse_y, coarse_z, 2, 2, 2, fine_chans)
    lifted = jnp.transpose(lifted, (0, 3, 1, 4, 2, 5, 6)).reshape(2 * coarse_x, 2 * coarse_y, 2 * coarse_z, fine_chans)
    joined = jnp.concatenate([lifted, skip], axis=-1)
    return jax.nn.gelu(conv_same(joined, last_kernel)).astype(jnp.bfloat16)
```

```python
import functools

import jax
import jax.numpy as jnp
from jax import lax
from jax.experimental import pallas as pl
from jax.experimental.pallas import tpu as pltpu
from jax.sharding import PartitionSpec as P

MESH = pl.DeviceIdType.MESH
BF = jnp.bfloat16
F32 = jnp.float32


def gelu(v):
    return jax.nn.gelu(v, approximate=True)


def dot(a, b):
    return jnp.dot(a, b, preferred_element_type=F32)


def z_shifted(v, shift):
    if shift == 0:
        return v
    depth = v.shape[-2]
    rolled = pltpu.roll(v, (-shift) % depth, axis=v.ndim - 2)
    at = lax.broadcasted_iota(jnp.int32, v.shape, v.ndim - 2)
    edge = depth - 1 if shift > 0 else 0
    return jnp.where(at == edge, 0.0, rolled)


def kernel(
    sizes,
    vol_ref, first_ref, down_hbm, mid_hbm, up_hbm, last_ref,
    out_ref,
    vol_pair, vol_taps, first_w, last_w, down_ref, mid_ref, up_ref,
    joined, joined_taps, acc, coarse_pad, coarse_own, coarse_taps,
    middle_out, middle_all, piece_out, piece_all,
    local_sem, w_send, w_recv, relay_send, relay_recv,
    halo_send, halo_recv, pair_send, pair_recv,
    coarse_send, coarse_recv, mid_send, mid_recv,
):
    R, Q, D = sizes
    r, q, c = lax.axis_index("row"), lax.axis_index("col"), lax.axis_index("depth")
    X, Y, Z, C = vol_ref.shape
    ZF = Z * D
    half = C // D
    hx, hy, hz = X // 2, Y // 2, ZF // 2
    wide = down_hbm.shape[2]
    wm = mid_hbm.shape[2]
    group = 9
    parity = q % 2
    lane0 = pl.multiple_of(c * half, half)

    def remote(src, dst, ssem, rsem, dev):
        return pltpu.make_async_remote_copy(
            src_ref=src, dst_ref=dst, send_sem=ssem, recv_sem=rsem,
            device_id=dev, device_id_type=MESH,
        )

    local = [
        pltpu.make_async_copy(down_hbm, down_ref, local_sem.at[0]),
        pltpu.make_async_copy(mid_hbm, mid_ref, local_sem.at[1]),
        pltpu.make_async_copy(up_hbm, up_ref, local_sem.at[2]),
    ]
    shards = []
    for slot, (shard, gathered) in enumerate(((first_ref, first_w), (last_ref, last_w))):
        rows = shard.shape[1]
        own = pl.ds(pl.multiple_of(r * rows, rows), rows)
        shards.append(pltpu.make_async_copy(
            shard.at[:, :, pl.ds(lane0, half)], gathered.at[:, own, :], local_sem.at[3 + slot]))
    zero_c = jnp.zeros(vol_pair.shape[1:], BF)
    for d in range(D):
        vol_pair[d] = zero_c
    joined[...] = jnp.zeros(joined.shape, BF)
    coarse_pad[...] = jnp.zeros(coarse_pad.shape, BF)
    vol_pair[c, 1:X + 1, 1:Y + 1] = vol_ref[...]

    barrier = pltpu.get_barrier_semaphore()
    for k in range(1, R):
        pl.semaphore_signal(barrier, inc=1, device_id=((r + k) % R, q, c), device_id_type=MESH)
    for k in range(1, D):
        pl.semaphore_signal(barrier, inc=1, device_id=(r, q, (c + k) % D), device_id_type=MESH)
    for dx in (-1, 0, 1):
        for k in range(1, Q):
            def greet(dx=dx, k=k):
                pl.semaphore_signal(
                    barrier, inc=1, device_id=(r + dx, (q + k) % Q, c), device_id_type=MESH)
            if dx == 0:
                greet()
            else:
                pl.when((r + dx >= 0) & (r + dx < R))(greet)
    sides = jnp.where(r > 0, 1, 0) + jnp.where(r < R - 1, 1, 0)
    pl.semaphore_wait(barrier, (R - 1) + (D - 1) + (1 + sides) * (Q - 1))

    for copy in local + shards:
        copy.start()

    def halo(buf, lanes, slot, start):
        n = 0
        for dx in (-1, 0, 1):
            for dy in (-1, 0, 1):
                if dx == 0 and dy == 0:
                    continue
                sx = {1: pl.ds(X, 1), -1: pl.ds(1, 1), 0: pl.ds(1, X)}[dx]
                tx = {1: pl.ds(0, 1), -1: pl.ds(X + 1, 1), 0: pl.ds(1, X)}[dx]
                sy = {1: pl.ds(Y, 1), -1: pl.ds(1, 1), 0: pl.ds(1, Y)}[dy]
                ty = {1: pl.ds(0, 1), -1: pl.ds(Y + 1, 1), 0: pl.ds(1, Y)}[dy]
                copy = remote(
                    buf.at[sx, sy, :, lanes], buf.at[tx, ty, :, lanes],
                    halo_send.at[slot, n], halo_recv.at[slot, n], (r + dx, q + dy, c))
                to = (r + dx >= 0) & (r + dx < R) & (q + dy >= 0) & (q + dy < Q)
                come = (r - dx >= 0) & (r - dx < R) & (q - dy >= 0) & (q - dy < Q)
                if start:
                    pl.when(to)(copy.start)
                else:
                    pl.when(come)(copy.wait_recv)
                    pl.when(to)(copy.wait_send)
                n += 1

    everything = pl.ds(0, C)
    halo(vol_pair.at[c], everything, 0, True)

    def spread(shard, gathered, slot):
        rows = shard.shape[1]
        own = pl.ds(pl.multiple_of(r * rows, rows), rows)
        taps = pl.ds(group * parity, 2 * group)
        return [
            remote(
                shard.at[taps, :, pl.ds(lane0, half)], gathered.at[taps, own, :],
                w_send.at[slot, k], w_recv.at[slot, k], ((r + k) % R, q, c))
            for k in range(1, R)
        ]

    def relays(shard, gathered, slot):
        rows = shard.shape[1]
        taps = pl.ds(2 * group * parity, group)
        other = q + 1 - 2 * parity
        out = []
        for k in range(1, R):
            origin = (r + R - k) % R
            at = pl.ds(pl.multiple_of(origin * rows, rows), rows)
            out.append(remote(
                gathered.at[taps, at, :], gathered.at[taps, at, :],
                relay_send.at[slot, k], relay_recv.at[slot, k], (r, other, c)))
        return out

    first_out, last_out = spread(first_ref, first_w, 0), spread(last_ref, last_w, 1)
    first_relay, last_relay = relays(first_ref, first_w, 0), relays(last_ref, last_w, 1)
    for copy in first_out:
        copy.start()

    halo(vol_pair.at[c], everything, 0, False)

    def pair_copy(src, dst, slot, k):
        return remote(src, dst, pair_send.at[slot, k], pair_recv.at[slot, k], (r, q, (c + k) % D))

    vols = [pair_copy(vol_pair.at[c], vol_pair.at[c], 0, k) for k in range(1, D)]
    for copy in vols:
        copy.start()
    for copy in vols:
        copy.wait_recv()

    def build_taps(get, taps_ref, chans, width):
        for x in range(taps_ref.shape[0]):
            v = get(x)
            for s in range(3):
                taps_ref[x, :, :, s * width + chans.start:s * width + chans.stop] = (
                    z_shifted(v, s - 1).astype(taps_ref.dtype))

    def vol_plane(x):
        return jnp.concatenate([vol_pair[d, x].astype(F32) for d in range(D)], axis=1)

    build_taps(vol_plane, vol_taps, slice(0, C), C)

    for copy, relay in zip(first_out, first_relay):
        copy.wait_recv()
        relay.start()
    for copy in last_out:
        copy.start()
    shards[0].wait()
    for relay in first_relay:
        relay.wait_recv()

    def conv(taps_ref, weights):
        chans = weights.shape[1]
        for ab in range(9):
            a, b = ab // 3, ab % 3
            rhs = weights[3 * ab:3 * ab + 3].reshape(3 * chans, weights.shape[2])
            for x in range(X):
                lhs = taps_ref[x + a, b:b + Y].reshape(Y * ZF, 3 * chans)
                part = dot(lhs, rhs)
                if ab == 0:
                    acc[x] = part
                else:
                    acc[x] += part

    conv(vol_taps, first_w)
    skip_lanes = pl.ds(pl.multiple_of(C + c * half, half), half)
    for x in range(X):
        joined[x + 1, 1:Y + 1, :, skip_lanes] = gelu(acc[x]).astype(BF).reshape(Y, ZF, half)
    inside = joined.at[pl.ds(1, X), pl.ds(1, Y), :, skip_lanes]
    skips = [pair_copy(inside, inside, 1, k) for k in range(1, D)]
    for copy in skips:
        copy.start()
    for copy in skips:
        copy.wait_recv()
    upper = pl.ds(C, C)
    halo(joined, upper, 1, True)

    local[0].wait()
    fine_rows, coarse_rows = hy * ZF, hy * hz
    rows_c = lax.broadcasted_iota(jnp.int32, (coarse_rows, fine_rows), 0)
    rows_f = lax.broadcasted_iota(jnp.int32, (coarse_rows, fine_rows), 1)
    pick = [jnp.where(rows_f == 2 * rows_c + s, 1.0, 0.0).astype(BF) for s in range(2)]
    for i in range(hx):
        total = jnp.zeros((coarse_rows, wide), F32)
        for a in range(2):
            for b in range(2):
                rows = jnp.concatenate(
                    [joined[1 + 2 * i + a, 1 + 2 * j + b, :, C:2 * C] for j in range(hy)], axis=0)
                for s in range(2):
                    picked = dot(pick[s], rows).astype(BF)
                    total += dot(picked, down_ref[4 * a + 2 * b + s])
        coarse_own[i] = gelu(total).reshape(hy, hz, wide).astype(BF)

    sends = []
    for dx in (-1, 0, 1):
        src = {1: pl.ds(hx - 1, 1), -1: pl.ds(0, 1), 0: pl.ds(0, hx)}[dx]
        dst = {1: pl.ds(0, 1), -1: pl.ds(hx + 1, 1), 0: pl.ds(1, hx)}[dx]
        for k in range(Q):
            if dx == 0 and k == 0:
                continue
            at = pl.ds(1 + q * hy, hy)
            copy = remote(
                coarse_own.at[src], coarse_pad.at[dst, at],
                coarse_send.at[dx + 1, k], coarse_recv.at[dx + 1, k], (r + dx, (q + k) % Q, c))
            to = (r + dx >= 0) & (r + dx < R)
            come = (r - dx >= 0) & (r - dx < R)
            sends.append((dx, copy, to, come))
    for dx, copy, to, come in sends:
        if dx == 0:
            copy.start()
        else:
            pl.when(to)(copy.start)
    coarse_pad[1:1 + hx, pl.ds(1 + q * hy, hy)] = coarse_own[...]
    for dx, copy, to, come in sends:
        if dx == 0:
            copy.wait_recv()
        else:
            pl.when(come)(copy.wait_recv)
    build_taps(lambda x: coarse_pad[x].astype(F32), coarse_taps, slice(0, wide), wide)

    local[1].wait()
    slab = Q * hy
    for i in range(hx):
        total = jnp.zeros((slab * hz, wm), F32)
        for ab in range(9):
            a, b = ab // 3, ab % 3
            lhs = coarse_taps[i + a, b:b + slab].reshape(slab * hz, 3 * wide).astype(BF)
            total += dot(lhs, mid_ref[3 * ab:3 * ab + 3].reshape(3 * wide, wm))
        middle = gelu(total).astype(BF)
        for part in range(Q):
            middle_out[part, i] = middle[part * coarse_rows:(part + 1) * coarse_rows]
    mids = []
    for k in range(1, Q):
        target = (q + k) % Q
        mids.append(remote(
            middle_out.at[target], middle_all.at[q], mid_send.at[k], mid_recv.at[k],
            (r, target, c)))
    for copy in mids:
        copy.start()
    middle_all[q] = middle_out[q]

    for copy, relay in zip(last_out, last_relay):
        copy.wait_recv()
        relay.start()

    halo(joined, upper, 1, False)
    for x in range(X + 2):
        v = joined[x, :, :, C:2 * C].astype(F32)
        for s in range(3):
            joined_taps[x, :, :, s * 2 * C + C:(s + 1) * 2 * C] = z_shifted(v, s - 1).astype(BF)

    for copy in mids:
        copy.wait_recv()
    local[2].wait()
    rows_f = lax.broadcasted_iota(jnp.int32, (fine_rows, coarse_rows), 0)
    rows_c = lax.broadcasted_iota(jnp.int32, (fine_rows, coarse_rows), 1)
    place = [jnp.where(rows_f == 2 * rows_c + s, 1.0, 0.0).astype(BF) for s in range(2)]
    for i in range(hx):
        spread_rows = [
            [dot(place[s], middle_all[part, i]).astype(BF) for s in range(2)] for part in range(Q)]
        for a in range(2):
            for b in range(2):
                lifted = jnp.zeros((fine_rows, C), F32)
                for part in range(Q):
                    for s in range(2):
                        lifted += dot(
                            spread_rows[part][s],
                            up_ref[4 * a + 2 * b + s, part * wm:(part + 1) * wm])
                lifted = lifted.astype(BF)
                for j in range(hy):
                    joined[1 + 2 * i + a, 1 + 2 * j + b, :, 0:C] = lifted[j * ZF:(j + 1) * ZF]
    lower = pl.ds(0, C)
    halo(joined, lower, 2, True)
    shards[1].wait()
    for relay in last_relay:
        relay.wait_recv()
    halo(joined, lower, 2, False)
    for x in range(X + 2):
        v = joined[x, :, :, 0:C].astype(F32)
        for s in range(3):
            joined_taps[x, :, :, s * 2 * C:s * 2 * C + C] = z_shifted(v, s - 1).astype(BF)

    conv(joined_taps, last_w)
    for x in range(X):
        done = gelu(acc[x]).reshape(Y, D, Z, half)
        for d in range(D):
            piece_out[d, x] = done[:, d].astype(BF)
    pieces = []
    for k in range(1, D):
        target = (c + k) % D
        pieces.append(pair_copy(piece_out.at[target], piece_all.at[c], 2, k))
    for copy in pieces:
        copy.start()
    piece_all[c] = piece_out[c]
    for copy in pieces:
        copy.wait_recv()
    for d in range(D):
        out_ref[:, :, :, d * half:(d + 1) * half] = piece_all[d]

    for copy in first_out + last_out + first_relay + last_relay + vols + skips + mids + pieces:
        copy.wait_send()
    for dx, copy, to, come in sends:
        if dx == 0:
            copy.wait_send()
        else:
            pl.when(to)(copy.wait_send)


def body(sizes, volume, first_kernel, down_kernel, mid_kernel, up_kernel, last_kernel):
    R, Q, D = sizes
    X, Y, Z, C = volume.shape
    ZF, half = Z * D, C // D
    hx, hy, hz = X // 2, Y // 2, ZF // 2
    wide, wm = down_kernel.shape[2], mid_kernel.shape[2]
    slab = Q * hy
    DMA = pltpu.SemaphoreType.DMA
    vmem = pl.BlockSpec(memory_space=pltpu.VMEM)
    hbm = pl.BlockSpec(memory_space=pl.ANY)
    return pl.pallas_call(
        functools.partial(kernel, sizes),
        out_shape=jax.ShapeDtypeStruct(volume.shape, BF),
        in_specs=[vmem] + [hbm] * 5,
        out_specs=vmem,
        scratch_shapes=[
            pltpu.VMEM((D, X + 2, Y + 2, Z, C), BF),
            pltpu.VMEM((X + 2, Y + 2, ZF, 3 * C), BF),
            pltpu.VMEM((27, C, half), BF),
            pltpu.VMEM((27, 2 * C, half), BF),
            pltpu.VMEM(down_kernel.shape, BF),
            pltpu.VMEM(mid_kernel.shape, BF),
            pltpu.VMEM(up_kernel.shape, BF),
            pltpu.VMEM((X + 2, Y + 2, ZF, 2 * C), BF),
            pltpu.VMEM((X + 2, Y + 2, ZF, 6 * C), BF),
            pltpu.VMEM((X, Y * ZF, half), F32),
            pltpu.VMEM((hx + 2, slab + 2, hz, wide), BF),
            pltpu.VMEM((hx, hy, hz, wide), BF),
            pltpu.VMEM((hx + 2, slab + 2, hz, 3 * wide), F32),
            pltpu.VMEM((Q, hx, hy * hz, wm), BF),
            pltpu.VMEM((Q, hx, hy * hz, wm), BF),
            pltpu.VMEM((D, X, Y, Z, half), BF),
            pltpu.VMEM((D, X, Y, Z, half), BF),
            DMA((5,)),
            DMA((2, R)), DMA((2, R)), DMA((2, R)), DMA((2, R)),
            DMA((3, 8)), DMA((3, 8)),
            DMA((3, D)), DMA((3, D)),
            DMA((3, Q)), DMA((3, Q)),
            DMA((Q,)), DMA((Q,)),
        ],
        compiler_params=pltpu.CompilerParams(
            collective_id=0, has_side_effects=True, vmem_limit_bytes=60 * 1024 * 1024),
        name="unet",
    )(volume, first_kernel, down_kernel, mid_kernel, up_kernel, last_kernel)


def solution(mesh):
    sizes = tuple(mesh.shape[name] for name in ("row", "col", "depth"))
    placed = (
        P("row", "col", "depth", None),
        P(None, "row", None),
        P(),
        P(None, None, "col"),
        P(),
        P(None, "row", None),
    )
    return jax.shard_map(
        functools.partial(body, sizes), mesh=mesh, in_specs=placed,
        out_specs=P("row", "col", "depth", None), check_vma=False,
    )
```

```python
import functools

import jax
import jax.numpy as jnp
from jax import lax
from jax.experimental import pallas as pl
from jax.experimental.pallas import tpu as pltpu
from jax.sharding import PartitionSpec as P

MESH = pl.DeviceIdType.MESH
BF = jnp.bfloat16
F32 = jnp.float32


def gelu(v):
    return jax.nn.gelu(v, approximate=True)


def dot(a, b):
    return jnp.dot(a, b, preferred_element_type=F32)


def z_shifted(v, shift):
    if shift == 0:
        return v
    depth = v.shape[-2]
    rolled = pltpu.roll(v, (-shift) % depth, axis=v.ndim - 2)
    at = lax.broadcasted_iota(jnp.int32, v.shape, v.ndim - 2)
    edge = depth - 1 if shift > 0 else 0
    return jnp.where(at == edge, 0.0, rolled)


def kernel(
    sizes,
    vol_ref, first_ref, down_hbm, mid_hbm, up_hbm, last_ref,
    out_ref,
    vol_pair, vol_taps, first_w, last_w, down_ref, mid_ref, up_ref,
    joined, joined_taps, acc, coarse_pad, coarse_own, coarse_taps,
    middle_out, middle_all, piece_out, piece_all,
    local_sem, w_send, w_recv, x_send, x_recv, relay_send, relay_recv,
    halo_send, halo_recv, pair_send, pair_recv,
    coarse_send, coarse_recv, mid_send, mid_recv,
):
    R, Q, D = sizes
    r, q, c = lax.axis_index("row"), lax.axis_index("col"), lax.axis_index("depth")
    X, Y, Z, C = vol_ref.shape
    ZF = Z * D
    half = C // D
    hx, hy, hz = X // 2, Y // 2, ZF // 2
    wide = down_hbm.shape[2]
    wm = mid_hbm.shape[2]
    group = 9
    parity = q % 2
    lane0 = pl.multiple_of(c * half, half)

    def remote(src, dst, ssem, rsem, dev):
        return pltpu.make_async_remote_copy(
            src_ref=src, dst_ref=dst, send_sem=ssem, recv_sem=rsem,
            device_id=dev, device_id_type=MESH,
        )

    local = [
        pltpu.make_async_copy(down_hbm, down_ref, local_sem.at[0]),
        pltpu.make_async_copy(mid_hbm, mid_ref, local_sem.at[1]),
        pltpu.make_async_copy(up_hbm, up_ref, local_sem.at[2]),
    ]
    shards = []
    for slot, (shard, gathered) in enumerate(((first_ref, first_w), (last_ref, last_w))):
        rows = shard.shape[1]
        own = pl.ds(pl.multiple_of(r * rows, rows), rows)
        shards.append(pltpu.make_async_copy(
            shard.at[:, :, pl.ds(lane0, half)], gathered.at[:, own, :], local_sem.at[3 + slot]))
    zero_c = jnp.zeros(vol_pair.shape[1:], BF)
    for d in range(D):
        vol_pair[d] = zero_c
    joined[...] = jnp.zeros(joined.shape, BF)
    coarse_pad[...] = jnp.zeros(coarse_pad.shape, BF)
    vol_pair[c, 1:X + 1, 1:Y + 1] = vol_ref[...]

    barrier = pltpu.get_barrier_semaphore()
    for k in range(1, R):
        pl.semaphore_signal(barrier, inc=1, device_id=((r + k) % R, q, c), device_id_type=MESH)
    for k in range(1, D):
        pl.semaphore_signal(barrier, inc=1, device_id=(r, q, (c + k) % D), device_id_type=MESH)
    for dx in (-1, 0, 1):
        for k in range(1, Q):
            def greet(dx=dx, k=k):
                pl.semaphore_signal(
                    barrier, inc=1, device_id=(r + dx, (q + k) % Q, c), device_id_type=MESH)
            if dx == 0:
                greet()
            else:
                pl.when((r + dx >= 0) & (r + dx < R))(greet)
    sides = jnp.where(r > 0, 1, 0) + jnp.where(r < R - 1, 1, 0)
    pl.semaphore_wait(barrier, (R - 1) + (D - 1) + (1 + sides) * (Q - 1))

    for copy in local + shards:
        copy.start()

    def halo(buf, lanes, slot, start):
        n = 0
        for dx in (-1, 0, 1):
            for dy in (-1, 0, 1):
                if dx == 0 and dy == 0:
                    continue
                sx = {1: pl.ds(X, 1), -1: pl.ds(1, 1), 0: pl.ds(1, X)}[dx]
                tx = {1: pl.ds(0, 1), -1: pl.ds(X + 1, 1), 0: pl.ds(1, X)}[dx]
                sy = {1: pl.ds(Y, 1), -1: pl.ds(1, 1), 0: pl.ds(1, Y)}[dy]
                ty = {1: pl.ds(0, 1), -1: pl.ds(Y + 1, 1), 0: pl.ds(1, Y)}[dy]
                copy = remote(
                    buf.at[sx, sy, :, lanes], buf.at[tx, ty, :, lanes],
                    halo_send.at[slot, n], halo_recv.at[slot, n], (r + dx, q + dy, c))
                to = (r + dx >= 0) & (r + dx < R) & (q + dy >= 0) & (q + dy < Q)
                come = (r - dx >= 0) & (r - dx < R) & (q - dy >= 0) & (q - dy < Q)
                if start:
                    pl.when(to)(copy.start)
                else:
                    pl.when(come)(copy.wait_recv)
                    pl.when(to)(copy.wait_send)
                n += 1

    everything = pl.ds(0, C)
    halo(vol_pair.at[c], everything, 0, True)

    inner, outer = r % 2, R // 2
    pair_row, pair_col = r + 1 - 2 * inner, q + 1 - 2 * parity
    most, rest = pl.ds(group * parity, 2 * group), pl.ds(2 * group * parity, group)
    part = last_ref.shape[1] // 2
    blocks = (
        (first_ref, first_w, 0, first_ref.shape[1]),
        (last_ref, last_w, 0, part),
        (last_ref, last_w, part, part),
    )

    def rows_at(n, origin):
        shard, _, low, count = blocks[n]
        return pl.ds(pl.multiple_of(origin * shard.shape[1] + low, count), count)

    def origin_of(k, side):
        return (r + R - 2 * k) % R - inner + side

    def leg(n, step):
        shard, gathered, low, count = blocks[n]
        mine = shard.at[most, pl.ds(low, count), pl.ds(lane0, half)]
        out = []
        if step == 0:
            at = rows_at(n, r)
            for k in range(1, outer):
                out.append(remote(
                    mine, gathered.at[most, at, :], w_send.at[n, k], w_recv.at[n, k],
                    ((r + 2 * k) % R, q, c)))
        elif step == 1:
            for k in range(outer):
                at = rows_at(n, origin_of(k, inner))
                out.append(remote(
                    mine if k == 0 else gathered.at[most, at, :], gathered.at[most, at, :],
                    x_send.at[n, k], x_recv.at[n, k], (pair_row, q, c)))
        else:
            for slot in range(1, 2 * outer):
                k, side = slot % outer, (inner if slot < outer else 1 - inner)
                at = rows_at(n, origin_of(k, side))
                out.append(remote(
                    gathered.at[rest, at, :], gathered.at[rest, at, :],
                    relay_send.at[n, slot], relay_recv.at[n, slot], (r, pair_col, c)))
        return out

    legs = [[leg(n, step) for step in range(3)] for n in range(3)]

    def go(n, step):
        first_leg, second_leg, third_leg = legs[n]
        if step == 0:
            for copy in first_leg:
                copy.start()
        elif step == 1:
            second_leg[0].start()
            for k in range(1, outer):
                first_leg[k - 1].wait_recv()
                second_leg[k].start()
        elif step == 2:
            for k in range(1, outer):
                third_leg[k - 1].start()
            for k in range(outer):
                second_leg[k].wait_recv()
                third_leg[outer - 1 + k].start()
        else:
            for copy in third_leg:
                copy.wait_recv()

    go(0, 0)

    halo(vol_pair.at[c], everything, 0, False)

    def pair_copy(src, dst, slot, k):
        return remote(src, dst, pair_send.at[slot, k], pair_recv.at[slot, k], (r, q, (c + k) % D))

    vols = [pair_copy(vol_pair.at[c], vol_pair.at[c], 0, k) for k in range(1, D)]
    for copy in vols:
        copy.start()
    for copy in vols:
        copy.wait_recv()

    def build_taps(get, taps_ref, chans, width):
        for x in range(taps_ref.shape[0]):
            v = get(x)
            for s in range(3):
                taps_ref[x, :, :, s * width + chans.start:s * width + chans.stop] = (
                    z_shifted(v, s - 1).astype(taps_ref.dtype))

    def vol_plane(x):
        return jnp.concatenate([vol_pair[d, x].astype(F32) for d in range(D)], axis=1)

    build_taps(vol_plane, vol_taps, slice(0, C), C)

    go(0, 1)
    go(1, 0)
    go(2, 0)
    go(0, 2)
    shards[0].wait()
    go(0, 3)

    def conv(taps_ref, weights):
        chans = weights.shape[1]
        for ab in range(9):
            a, b = ab // 3, ab % 3
            rhs = weights[3 * ab:3 * ab + 3].reshape(3 * chans, weights.shape[2])
            for x in range(X):
                lhs = taps_ref[x + a, b:b + Y].reshape(Y * ZF, 3 * chans)
                part = dot(lhs, rhs)
                if ab == 0:
                    acc[x] = part
                else:
                    acc[x] += part

    conv(vol_taps, first_w)
    skip_lanes = pl.ds(pl.multiple_of(C + c * half, half), half)
    for x in range(X):
        joined[x + 1, 1:Y + 1, :, skip_lanes] = gelu(acc[x]).astype(BF).reshape(Y, ZF, half)
    inside = joined.at[pl.ds(1, X), pl.ds(1, Y), :, skip_lanes]
    skips = [pair_copy(inside, inside, 1, k) for k in range(1, D)]
    for copy in skips:
        copy.start()
    for copy in skips:
        copy.wait_recv()
    upper = pl.ds(C, C)
    go(1, 1)

    local[0].wait()
    fine_rows, coarse_rows = hy * ZF, hy * hz
    rows_c = lax.broadcasted_iota(jnp.int32, (coarse_rows, fine_rows), 0)
    rows_f = lax.broadcasted_iota(jnp.int32, (coarse_rows, fine_rows), 1)
    pick = [jnp.where(rows_f == 2 * rows_c + s, 1.0, 0.0).astype(BF) for s in range(2)]
    for i in range(hx):
        total = jnp.zeros((coarse_rows, wide), F32)
        for a in range(2):
            for b in range(2):
                rows = jnp.concatenate(
                    [joined[1 + 2 * i + a, 1 + 2 * j + b, :, C:2 * C] for j in range(hy)], axis=0)
                for s in range(2):
                    picked = dot(pick[s], rows).astype(BF)
                    total += dot(picked, down_ref[4 * a + 2 * b + s])
        coarse_own[i] = gelu(total).reshape(hy, hz, wide).astype(BF)

    sends = []
    for dx in (-1, 0, 1):
        src = {1: pl.ds(hx - 1, 1), -1: pl.ds(0, 1), 0: pl.ds(0, hx)}[dx]
        dst = {1: pl.ds(0, 1), -1: pl.ds(hx + 1, 1), 0: pl.ds(1, hx)}[dx]
        for k in range(Q):
            if dx == 0 and k == 0:
                continue
            at = pl.ds(1 + q * hy, hy)
            copy = remote(
                coarse_own.at[src], coarse_pad.at[dst, at],
                coarse_send.at[dx + 1, k], coarse_recv.at[dx + 1, k], (r + dx, (q + k) % Q, c))
            to = (r + dx >= 0) & (r + dx < R)
            come = (r - dx >= 0) & (r - dx < R)
            sends.append((dx, copy, to, come))
    for dx, copy, to, come in sends:
        if dx == 0:
            copy.start()
        else:
            pl.when(to)(copy.start)
    coarse_pad[1:1 + hx, pl.ds(1 + q * hy, hy)] = coarse_own[...]
    halo(joined, upper, 1, True)
    go(1, 2)
    for dx, copy, to, come in sends:
        if dx == 0:
            copy.wait_recv()
        else:
            pl.when(come)(copy.wait_recv)
    go(2, 1)
    build_taps(lambda x: coarse_pad[x].astype(F32), coarse_taps, slice(0, wide), wide)

    local[1].wait()
    slab = Q * hy
    for i in range(hx):
        total = jnp.zeros((slab * hz, wm), F32)
        for ab in range(9):
            a, b = ab // 3, ab % 3
            lhs = coarse_taps[i + a, b:b + slab].reshape(slab * hz, 3 * wide).astype(BF)
            total += dot(lhs, mid_ref[3 * ab:3 * ab + 3].reshape(3 * wide, wm))
        middle = gelu(total).astype(BF)
        for part in range(Q):
            middle_out[part, i] = middle[part * coarse_rows:(part + 1) * coarse_rows]
    mids = []
    for k in range(1, Q):
        target = (q + k) % Q
        mids.append(remote(
            middle_out.at[target], middle_all.at[q], mid_send.at[k], mid_recv.at[k],
            (r, target, c)))
    for copy in mids:
        copy.start()
    middle_all[q] = middle_out[q]

    go(2, 2)
    halo(joined, upper, 1, False)
    for x in range(X + 2):
        v = joined[x, :, :, C:2 * C].astype(F32)
        for s in range(3):
            joined_taps[x, :, :, s * 2 * C + C:(s + 1) * 2 * C] = z_shifted(v, s - 1).astype(BF)

    for copy in mids:
        copy.wait_recv()
    local[2].wait()
    rows_f = lax.broadcasted_iota(jnp.int32, (fine_rows, coarse_rows), 0)
    rows_c = lax.broadcasted_iota(jnp.int32, (fine_rows, coarse_rows), 1)
    place = [jnp.where(rows_f == 2 * rows_c + s, 1.0, 0.0).astype(BF) for s in range(2)]
    for i in range(hx):
        spread_rows = [
            [dot(place[s], middle_all[part, i]).astype(BF) for s in range(2)] for part in range(Q)]
        for a in range(2):
            for b in range(2):
                lifted = jnp.zeros((fine_rows, C), F32)
                for part in range(Q):
                    for s in range(2):
                        lifted += dot(
                            spread_rows[part][s],
                            up_ref[4 * a + 2 * b + s, part * wm:(part + 1) * wm])
                lifted = lifted.astype(BF)
                for j in range(hy):
                    joined[1 + 2 * i + a, 1 + 2 * j + b, :, 0:C] = lifted[j * ZF:(j + 1) * ZF]
    lower = pl.ds(0, C)
    halo(joined, lower, 2, True)
    shards[1].wait()
    go(1, 3)
    go(2, 3)
    halo(joined, lower, 2, False)
    for x in range(X + 2):
        v = joined[x, :, :, 0:C].astype(F32)
        for s in range(3):
            joined_taps[x, :, :, s * 2 * C:s * 2 * C + C] = z_shifted(v, s - 1).astype(BF)

    conv(joined_taps, last_w)
    for x in range(X):
        done = gelu(acc[x]).reshape(Y, D, Z, half)
        for d in range(D):
            piece_out[d, x] = done[:, d].astype(BF)
    pieces = []
    for k in range(1, D):
        target = (c + k) % D
        pieces.append(pair_copy(piece_out.at[target], piece_all.at[c], 2, k))
    for copy in pieces:
        copy.start()
    piece_all[c] = piece_out[c]
    for copy in pieces:
        copy.wait_recv()
    for d in range(D):
        out_ref[:, :, :, d * half:(d + 1) * half] = piece_all[d]

    for copy in [copy for block in legs for step in block for copy in step] + vols + skips + mids + pieces:
        copy.wait_send()
    for dx, copy, to, come in sends:
        if dx == 0:
            copy.wait_send()
        else:
            pl.when(to)(copy.wait_send)


def body(sizes, volume, first_kernel, down_kernel, mid_kernel, up_kernel, last_kernel):
    R, Q, D = sizes
    X, Y, Z, C = volume.shape
    ZF, half = Z * D, C // D
    hx, hy, hz = X // 2, Y // 2, ZF // 2
    wide, wm = down_kernel.shape[2], mid_kernel.shape[2]
    slab = Q * hy
    DMA = pltpu.SemaphoreType.DMA
    vmem = pl.BlockSpec(memory_space=pltpu.VMEM)
    hbm = pl.BlockSpec(memory_space=pl.ANY)
    return pl.pallas_call(
        functools.partial(kernel, sizes),
        out_shape=jax.ShapeDtypeStruct(volume.shape, BF),
        in_specs=[vmem] + [hbm] * 5,
        out_specs=vmem,
        scratch_shapes=[
            pltpu.VMEM((D, X + 2, Y + 2, Z, C), BF),
            pltpu.VMEM((X + 2, Y + 2, ZF, 3 * C), BF),
            pltpu.VMEM((27, C, half), BF),
            pltpu.VMEM((27, 2 * C, half), BF),
            pltpu.VMEM(down_kernel.shape, BF),
            pltpu.VMEM(mid_kernel.shape, BF),
            pltpu.VMEM(up_kernel.shape, BF),
            pltpu.VMEM((X + 2, Y + 2, ZF, 2 * C), BF),
            pltpu.VMEM((X + 2, Y + 2, ZF, 6 * C), BF),
            pltpu.VMEM((X, Y * ZF, half), F32),
            pltpu.VMEM((hx + 2, slab + 2, hz, wide), BF),
            pltpu.VMEM((hx, hy, hz, wide), BF),
            pltpu.VMEM((hx + 2, slab + 2, hz, 3 * wide), F32),
            pltpu.VMEM((Q, hx, hy * hz, wm), BF),
            pltpu.VMEM((Q, hx, hy * hz, wm), BF),
            pltpu.VMEM((D, X, Y, Z, half), BF),
            pltpu.VMEM((D, X, Y, Z, half), BF),
            DMA((5,)),
            DMA((3, R)), DMA((3, R)), DMA((3, R)), DMA((3, R)), DMA((3, R)), DMA((3, R)),
            DMA((3, 8)), DMA((3, 8)),
            DMA((3, D)), DMA((3, D)),
            DMA((3, Q)), DMA((3, Q)),
            DMA((Q,)), DMA((Q,)),
        ],
        compiler_params=pltpu.CompilerParams(
            collective_id=0, has_side_effects=True, vmem_limit_bytes=60 * 1024 * 1024),
        name="unet",
    )(volume, first_kernel, down_kernel, mid_kernel, up_kernel, last_kernel)


def solution(mesh):
    sizes = tuple(mesh.shape[name] for name in ("row", "col", "depth"))
    placed = (
        P("row", "col", "depth", None),
        P(None, "row", None),
        P(),
        P(None, None, "col"),
        P(),
        P(None, "row", None),
    )
    return jax.shard_map(
        functools.partial(body, sizes), mesh=mesh, in_specs=placed,
        out_specs=P("row", "col", "depth", None), check_vma=False,
    )
```

```python
import functools

import jax
import jax.numpy as jnp
from jax import lax
from jax.experimental import pallas as pl
from jax.experimental.pallas import tpu as pltpu
from jax.sharding import PartitionSpec as P

MESH = pl.DeviceIdType.MESH
BF = jnp.bfloat16
F32 = jnp.float32


def gelu(v):
    return jax.nn.gelu(v, approximate=True)


def dot(a, b):
    return jnp.dot(a, b, preferred_element_type=F32)


def z_shifted(v, shift):
    if shift == 0:
        return v
    depth = v.shape[-2]
    rolled = pltpu.roll(v, (-shift) % depth, axis=v.ndim - 2)
    at = lax.broadcasted_iota(jnp.int32, v.shape, v.ndim - 2)
    edge = depth - 1 if shift > 0 else 0
    return jnp.where(at == edge, 0.0, rolled)


def kernel(
    sizes,
    vol_ref, first_ref, down_hbm, mid_hbm, up_hbm, last_ref,
    out_ref,
    vol_pair, vol_taps, first_w, last_w, down_ref, mid_ref, up_ref,
    joined, joined_taps, acc, coarse_pad, coarse_own, coarse_taps,
    middle_out, middle_all, piece_out, piece_all,
    local_sem, w_send, w_recv, x_send, x_recv, relay_send, relay_recv,
    halo_send, halo_recv, pair_send, pair_recv,
    coarse_send, coarse_recv, mid_send, mid_recv,
):
    R, Q, D = sizes
    r, q, c = lax.axis_index("row"), lax.axis_index("col"), lax.axis_index("depth")
    X, Y, Z, C = vol_ref.shape
    ZF = Z * D
    half = C // D
    hx, hy, hz = X // 2, Y // 2, ZF // 2
    wide = down_hbm.shape[2]
    wm = mid_hbm.shape[2]
    group = 9
    parity = q % 2
    lane0 = pl.multiple_of(c * half, half)

    def remote(src, dst, ssem, rsem, dev):
        return pltpu.make_async_remote_copy(
            src_ref=src, dst_ref=dst, send_sem=ssem, recv_sem=rsem,
            device_id=dev, device_id_type=MESH,
        )

    local = [
        pltpu.make_async_copy(down_hbm, down_ref, local_sem.at[0]),
        pltpu.make_async_copy(mid_hbm, mid_ref, local_sem.at[1]),
        pltpu.make_async_copy(up_hbm, up_ref, local_sem.at[2]),
    ]
    shards = []
    for slot, (shard, gathered) in enumerate(((first_ref, first_w), (last_ref, last_w))):
        rows = shard.shape[1]
        own = pl.ds(pl.multiple_of(r * rows, rows), rows)
        shards.append(pltpu.make_async_copy(
            shard.at[:, :, pl.ds(lane0, half)], gathered.at[:, own, :], local_sem.at[3 + slot]))
    zero_c = jnp.zeros(vol_pair.shape[1:], BF)
    for d in range(D):
        vol_pair[d] = zero_c
    joined[...] = jnp.zeros(joined.shape, BF)
    coarse_pad[...] = jnp.zeros(coarse_pad.shape, BF)
    vol_pair[c, 1:X + 1, 1:Y + 1] = vol_ref[...]

    barrier = pltpu.get_barrier_semaphore()
    for k in range(1, R):
        pl.semaphore_signal(barrier, inc=1, device_id=((r + k) % R, q, c), device_id_type=MESH)
    for k in range(1, D):
        pl.semaphore_signal(barrier, inc=1, device_id=(r, q, (c + k) % D), device_id_type=MESH)
    for dx in (-1, 0, 1):
        for k in range(1, Q):
            def greet(dx=dx, k=k):
                pl.semaphore_signal(
                    barrier, inc=1, device_id=(r + dx, (q + k) % Q, c), device_id_type=MESH)
            if dx == 0:
                greet()
            else:
                pl.when((r + dx >= 0) & (r + dx < R))(greet)
    sides = jnp.where(r > 0, 1, 0) + jnp.where(r < R - 1, 1, 0)
    pl.semaphore_wait(barrier, (R - 1) + (D - 1) + (1 + sides) * (Q - 1))

    for copy in local + shards:
        copy.start()

    def halo(buf, lanes, slot, start):
        n = 0
        for dx in (-1, 0, 1):
            for dy in (-1, 0, 1):
                if dx == 0 and dy == 0:
                    continue
                sx = {1: pl.ds(X, 1), -1: pl.ds(1, 1), 0: pl.ds(1, X)}[dx]
                tx = {1: pl.ds(0, 1), -1: pl.ds(X + 1, 1), 0: pl.ds(1, X)}[dx]
                sy = {1: pl.ds(Y, 1), -1: pl.ds(1, 1), 0: pl.ds(1, Y)}[dy]
                ty = {1: pl.ds(0, 1), -1: pl.ds(Y + 1, 1), 0: pl.ds(1, Y)}[dy]
                copy = remote(
                    buf.at[sx, sy, :, lanes], buf.at[tx, ty, :, lanes],
                    halo_send.at[slot, n], halo_recv.at[slot, n], (r + dx, q + dy, c))
                to = (r + dx >= 0) & (r + dx < R) & (q + dy >= 0) & (q + dy < Q)
                come = (r - dx >= 0) & (r - dx < R) & (q - dy >= 0) & (q - dy < Q)
                if start:
                    pl.when(to)(copy.start)
                else:
                    pl.when(come)(copy.wait_recv)
                    pl.when(to)(copy.wait_send)
                n += 1

    everything = pl.ds(0, C)
    halo(vol_pair.at[c], everything, 0, True)

    inner, outer = r % 2, R // 2
    pair_row, pair_col = r + 1 - 2 * inner, q + 1 - 2 * parity
    most, rest = pl.ds(group * parity, 2 * group), pl.ds(2 * group * parity, group)
    part = last_ref.shape[1] // 2
    blocks = (
        (first_ref, first_w, 0, first_ref.shape[1]),
        (last_ref, last_w, 0, part),
        (last_ref, last_w, part, part),
    )

    def rows_at(n, origin):
        shard, _, low, count = blocks[n]
        return pl.ds(pl.multiple_of(origin * shard.shape[1] + low, count), count)

    line = r // 2

    def arrives(way, s):
        return line - 1 - s >= 0 if way == 0 else line + 1 + s < outer

    def leaves(way, s):
        if way == 0:
            return (line - s >= 0) & (line + 1 < outer)
        return (line + s < outer) & (line - 1 >= 0)

    def origin_of(way, s, side):
        return 2 * (line - 1 - s if way == 0 else line + 1 + s) + side

    def hop(n, way, s):
        shard, gathered, low, count = blocks[n]
        origin = origin_of(way, s - 1, inner)
        at = rows_at(n, jnp.clip(origin, 0, R - 1))
        src = shard.at[most, pl.ds(low, count), pl.ds(lane0, half)] if s == 0 else (
            gathered.at[most, at, :])
        return remote(
            src, gathered.at[most, at, :], w_send.at[n, 2 * s + way], w_recv.at[n, 2 * s + way],
            (r + 2 - 4 * way, q, c))

    def across(n, way, s):
        shard, gathered, low, count = blocks[n]
        at = rows_at(n, jnp.clip(origin_of(way, s, inner), 0, R - 1))
        src = shard.at[most, pl.ds(low, count), pl.ds(lane0, half)] if s < 0 else (
            gathered.at[most, at, :])
        slot = 2 * s + way + 2
        return remote(
            src, gathered.at[most, at, :], x_send.at[n, slot], x_recv.at[n, slot],
            (pair_row, q, c))

    def over(n, way, s, other):
        _, gathered, _, _ = blocks[n]
        side = 1 - inner if other else inner
        at = rows_at(n, jnp.clip(origin_of(way, s, side), 0, R - 1))
        slot = 4 * s + 2 * way + other + 4
        return remote(
            gathered.at[rest, at, :], gathered.at[rest, at, :],
            relay_send.at[n, slot], relay_recv.at[n, slot], (r, pair_col, c))

    ways = [(way, s) for s in range(outer - 1) for way in range(2)]

    def begin(n):
        for way in range(2):
            pl.when(leaves(way, 0))(hop(n, way, 0).start)
        across(n, 0, -1).start()

    def forward(n, steps):
        for s in steps:
            for way in range(2):
                @pl.when(arrives(way, s))
                def _(way=way, s=s):
                    hop(n, way, s).wait_recv()
                if s + 1 < outer - 1:
                    pl.when(leaves(way, s + 1))(hop(n, way, s + 1).start)
                pl.when(arrives(way, s))(across(n, way, s).start)

    def share(n):
        for way, s in ways:
            pl.when(arrives(way, s))(over(n, way, s, 0).start)
        across(n, 0, -1).wait_recv()
        over(n, 0, -1, 1).start()
        for way, s in ways:
            @pl.when(arrives(way, s))
            def _(way=way, s=s):
                across(n, way, s).wait_recv()
                over(n, way, s, 1).start()

    def finish(n):
        over(n, 0, -1, 1).wait_recv()
        for way, s in ways:
            @pl.when(arrives(way, s))
            def _(way=way, s=s):
                over(n, way, s, 0).wait_recv()
                over(n, way, s, 1).wait_recv()

    def drain(n):
        across(n, 0, -1).wait_send()
        over(n, 0, -1, 1).wait_send()
        for way, s in ways:
            pl.when(leaves(way, s))(hop(n, way, s).wait_send)

            @pl.when(arrives(way, s))
            def _(way=way, s=s):
                across(n, way, s).wait_send()
                over(n, way, s, 0).wait_send()
                over(n, way, s, 1).wait_send()

    first_hop, later_hops = range(0, 1), range(1, outer - 1)

    begin(0)

    halo(vol_pair.at[c], everything, 0, False)

    def pair_copy(src, dst, slot, k):
        return remote(src, dst, pair_send.at[slot, k], pair_recv.at[slot, k], (r, q, (c + k) % D))

    vols = [pair_copy(vol_pair.at[c], vol_pair.at[c], 0, k) for k in range(1, D)]
    for copy in vols:
        copy.start()
    for copy in vols:
        copy.wait_recv()

    def build_taps(get, taps_ref, chans, width):
        for x in range(taps_ref.shape[0]):
            v = get(x)
            for s in range(3):
                taps_ref[x, :, :, s * width + chans.start:s * width + chans.stop] = (
                    z_shifted(v, s - 1).astype(taps_ref.dtype))

    def vol_plane(x):
        return jnp.concatenate([vol_pair[d, x].astype(F32) for d in range(D)], axis=1)

    build_taps(vol_plane, vol_taps, slice(0, C), C)

    forward(0, first_hop)
    forward(0, later_hops)
    begin(1)
    share(0)
    shards[0].wait()
    finish(0)
    forward(1, first_hop)
    begin(2)

    def conv(taps_ref, weights):
        chans = weights.shape[1]
        for ab in range(9):
            a, b = ab // 3, ab % 3
            rhs = weights[3 * ab:3 * ab + 3].reshape(3 * chans, weights.shape[2])
            for x in range(X):
                lhs = taps_ref[x + a, b:b + Y].reshape(Y * ZF, 3 * chans)
                part = dot(lhs, rhs)
                if ab == 0:
                    acc[x] = part
                else:
                    acc[x] += part

    conv(vol_taps, first_w)
    skip_lanes = pl.ds(pl.multiple_of(C + c * half, half), half)
    for x in range(X):
        joined[x + 1, 1:Y + 1, :, skip_lanes] = gelu(acc[x]).astype(BF).reshape(Y, ZF, half)
    inside = joined.at[pl.ds(1, X), pl.ds(1, Y), :, skip_lanes]
    skips = [pair_copy(inside, inside, 1, k) for k in range(1, D)]
    for copy in skips:
        copy.start()
    for copy in skips:
        copy.wait_recv()
    upper = pl.ds(C, C)
    forward(1, later_hops)

    local[0].wait()
    fine_rows, coarse_rows = hy * ZF, hy * hz
    rows_c = lax.broadcasted_iota(jnp.int32, (coarse_rows, fine_rows), 0)
    rows_f = lax.broadcasted_iota(jnp.int32, (coarse_rows, fine_rows), 1)
    pick = [jnp.where(rows_f == 2 * rows_c + s, 1.0, 0.0).astype(BF) for s in range(2)]
    for i in range(hx):
        total = jnp.zeros((coarse_rows, wide), F32)
        for a in range(2):
            for b in range(2):
                rows = jnp.concatenate(
                    [joined[1 + 2 * i + a, 1 + 2 * j + b, :, C:2 * C] for j in range(hy)], axis=0)
                for s in range(2):
                    picked = dot(pick[s], rows).astype(BF)
                    total += dot(picked, down_ref[4 * a + 2 * b + s])
        coarse_own[i] = gelu(total).reshape(hy, hz, wide).astype(BF)

    sends = []
    for dx in (-1, 0, 1):
        src = {1: pl.ds(hx - 1, 1), -1: pl.ds(0, 1), 0: pl.ds(0, hx)}[dx]
        dst = {1: pl.ds(0, 1), -1: pl.ds(hx + 1, 1), 0: pl.ds(1, hx)}[dx]
        for k in range(Q):
            if dx == 0 and k == 0:
                continue
            at = pl.ds(1 + q * hy, hy)
            copy = remote(
                coarse_own.at[src], coarse_pad.at[dst, at],
                coarse_send.at[dx + 1, k], coarse_recv.at[dx + 1, k], (r + dx, (q + k) % Q, c))
            to = (r + dx >= 0) & (r + dx < R)
            come = (r - dx >= 0) & (r - dx < R)
            sends.append((dx, copy, to, come))
    for dx, copy, to, come in sends:
        if dx == 0:
            copy.start()
        else:
            pl.when(to)(copy.start)
    coarse_pad[1:1 + hx, pl.ds(1 + q * hy, hy)] = coarse_own[...]
    halo(joined, upper, 1, True)
    share(1)
    forward(2, first_hop)
    for dx, copy, to, come in sends:
        if dx == 0:
            copy.wait_recv()
        else:
            pl.when(come)(copy.wait_recv)
    forward(2, later_hops)
    build_taps(lambda x: coarse_pad[x].astype(F32), coarse_taps, slice(0, wide), wide)

    local[1].wait()
    slab = Q * hy
    for i in range(hx):
        total = jnp.zeros((slab * hz, wm), F32)
        for ab in range(9):
            a, b = ab // 3, ab % 3
            lhs = coarse_taps[i + a, b:b + slab].reshape(slab * hz, 3 * wide).astype(BF)
            total += dot(lhs, mid_ref[3 * ab:3 * ab + 3].reshape(3 * wide, wm))
        middle = gelu(total).astype(BF)
        for part in range(Q):
            middle_out[part, i] = middle[part * coarse_rows:(part + 1) * coarse_rows]
    mids = []
    for k in range(1, Q):
        target = (q + k) % Q
        mids.append(remote(
            middle_out.at[target], middle_all.at[q], mid_send.at[k], mid_recv.at[k],
            (r, target, c)))
    for copy in mids:
        copy.start()
    middle_all[q] = middle_out[q]

    for copy in mids:
        copy.wait_recv()
    local[2].wait()
    rows_f = lax.broadcasted_iota(jnp.int32, (fine_rows, coarse_rows), 0)
    rows_c = lax.broadcasted_iota(jnp.int32, (fine_rows, coarse_rows), 1)
    place = [jnp.where(rows_f == 2 * rows_c + s, 1.0, 0.0).astype(BF) for s in range(2)]
    for i in range(hx):
        spread_rows = [
            [dot(place[s], middle_all[part, i]).astype(BF) for s in range(2)] for part in range(Q)]
        for a in range(2):
            for b in range(2):
                lifted = jnp.zeros((fine_rows, C), F32)
                for part in range(Q):
                    for s in range(2):
                        lifted += dot(
                            spread_rows[part][s],
                            up_ref[4 * a + 2 * b + s, part * wm:(part + 1) * wm])
                lifted = lifted.astype(BF)
                for j in range(hy):
                    joined[1 + 2 * i + a, 1 + 2 * j + b, :, 0:C] = lifted[j * ZF:(j + 1) * ZF]
    lower = pl.ds(0, C)
    halo(joined, lower, 2, True)
    share(2)
    halo(joined, upper, 1, False)
    for x in range(X + 2):
        v = joined[x, :, :, C:2 * C].astype(F32)
        for s in range(3):
            joined_taps[x, :, :, s * 2 * C + C:(s + 1) * 2 * C] = z_shifted(v, s - 1).astype(BF)

    shards[1].wait()
    finish(1)
    finish(2)
    halo(joined, lower, 2, False)
    for x in range(X + 2):
        v = joined[x, :, :, 0:C].astype(F32)
        for s in range(3):
            joined_taps[x, :, :, s * 2 * C:s * 2 * C + C] = z_shifted(v, s - 1).astype(BF)

    conv(joined_taps, last_w)
    for x in range(X):
        done = gelu(acc[x]).reshape(Y, D, Z, half)
        for d in range(D):
            piece_out[d, x] = done[:, d].astype(BF)
    pieces = []
    for k in range(1, D):
        target = (c + k) % D
        pieces.append(pair_copy(piece_out.at[target], piece_all.at[c], 2, k))
    for copy in pieces:
        copy.start()
    piece_all[c] = piece_out[c]
    for copy in pieces:
        copy.wait_recv()
    for d in range(D):
        out_ref[:, :, :, d * half:(d + 1) * half] = piece_all[d]

    for n in range(3):
        drain(n)
    for copy in vols + skips + mids + pieces:
        copy.wait_send()
    for dx, copy, to, come in sends:
        if dx == 0:
            copy.wait_send()
        else:
            pl.when(to)(copy.wait_send)


def body(sizes, volume, first_kernel, down_kernel, mid_kernel, up_kernel, last_kernel):
    R, Q, D = sizes
    X, Y, Z, C = volume.shape
    ZF, half = Z * D, C // D
    hx, hy, hz = X // 2, Y // 2, ZF // 2
    wide, wm = down_kernel.shape[2], mid_kernel.shape[2]
    slab = Q * hy
    DMA = pltpu.SemaphoreType.DMA
    vmem = pl.BlockSpec(memory_space=pltpu.VMEM)
    hbm = pl.BlockSpec(memory_space=pl.ANY)
    return pl.pallas_call(
        functools.partial(kernel, sizes),
        out_shape=jax.ShapeDtypeStruct(volume.shape, BF),
        in_specs=[vmem] + [hbm] * 5,
        out_specs=vmem,
        scratch_shapes=[
            pltpu.VMEM((D, X + 2, Y + 2, Z, C), BF),
            pltpu.VMEM((X + 2, Y + 2, ZF, 3 * C), BF),
            pltpu.VMEM((27, C, half), BF),
            pltpu.VMEM((27, 2 * C, half), BF),
            pltpu.VMEM(down_kernel.shape, BF),
            pltpu.VMEM(mid_kernel.shape, BF),
            pltpu.VMEM(up_kernel.shape, BF),
            pltpu.VMEM((X + 2, Y + 2, ZF, 2 * C), BF),
            pltpu.VMEM((X + 2, Y + 2, ZF, 6 * C), BF),
            pltpu.VMEM((X, Y * ZF, half), F32),
            pltpu.VMEM((hx + 2, slab + 2, hz, wide), BF),
            pltpu.VMEM((hx, hy, hz, wide), BF),
            pltpu.VMEM((hx + 2, slab + 2, hz, 3 * wide), F32),
            pltpu.VMEM((Q, hx, hy * hz, wm), BF),
            pltpu.VMEM((Q, hx, hy * hz, wm), BF),
            pltpu.VMEM((D, X, Y, Z, half), BF),
            pltpu.VMEM((D, X, Y, Z, half), BF),
            DMA((5,)),
            DMA((3, R)), DMA((3, R)), DMA((3, R)), DMA((3, R)), DMA((3, 2 * R)), DMA((3, 2 * R)),
            DMA((3, 8)), DMA((3, 8)),
            DMA((3, D)), DMA((3, D)),
            DMA((3, Q)), DMA((3, Q)),
            DMA((Q,)), DMA((Q,)),
        ],
        compiler_params=pltpu.CompilerParams(
            collective_id=0, has_side_effects=True, vmem_limit_bytes=60 * 1024 * 1024),
        name="unet",
    )(volume, first_kernel, down_kernel, mid_kernel, up_kernel, last_kernel)


def solution(mesh):
    sizes = tuple(mesh.shape[name] for name in ("row", "col", "depth"))
    placed = (
        P("row", "col", "depth", None),
        P(None, "row", None),
        P(),
        P(None, None, "col"),
        P(),
        P(None, "row", None),
    )
    return jax.shard_map(
        functools.partial(body, sizes), mesh=mesh, in_specs=placed,
        out_specs=P("row", "col", "depth", None), check_vma=False,
    )
```
